256 devices in a mesh: seq: 16 (over z_hi, x), dp: 8 (over y, core), head: 2 (over z_lo).
Axes of the slice: x: 4, y: 4, z: 8 (z_hi: 4, z_lo: 2; z = z_hi * 2 + z_lo), core: 2. Of those that a mesh axis runs over, the one named last changes fastest.
Arguments:
- queries: bfloat16 [8, 2048, 2048], P('dp', 'seq', 'head'), may hold values from -5 to 5
- keys: bfloat16 [8, 2048, 512], P('dp', 'seq', 'head'), may hold values from -5 to 5
- values: bfloat16 [8, 2048, 512], P('dp', 'seq', 'head'), may hold values from -4 to 4
- query_tangent: bfloat16 [8, 2048, 2048], P('dp', 'seq', 'head'), may hold values from -4 to 4
- key_tangent: bfloat16 [8, 2048, 512], P('dp', 'seq', 'head'), may hold values from -4 to 4
- value_tangent: bfloat16 [8, 2048, 512], P('dp', 'seq', 'head'), may hold values from -4 to 4
- lengths: int32 [8, 17], P('dp'), may hold values from 0 to 256, as said below
- out_weight: bfloat16 [2048, 4096], P('head'), may hold values from -0.125 to 0.125
- cotangent: bfloat16 [8, 2048, 4096], P('dp', 'seq'), may hold values from -0.0625 to 0.0625
Outputs:
- layer_tangent: bfloat16 [8, 2048, 4096], P('dp', 'seq', 'head')
- weight_hvp: float32 [4096, 2048], P(('seq', 'dp'), 'head')
The draws below stay inside these ranges and needn't reach their ends.
Inputs may be any that keep to these rules, and one draw needn't show every extreme that they name: `lengths`: each row sums to 2048; a length may be 0; in every row some document has exactly 256 tokens.
All inputs are finite; a program needn't handle non-finite values.
Results may differ from the reference program's by a relative error of at most 0.014.
Values may be sent and summed in bfloat16 or wider, within the bound.
A program may use at most 128 MiB of HBM per device.

```python
import jax
import jax.numpy as jnp
from jax import lax

D = 4096
HEADS = 16
KV_HEADS = 4
HEAD_DIM = 128
DOC_SHARDS = 2
SEQLEN = 2048
BATCH = 8
DOCMAX = 256
N_SEQ = 16


def doc_layout(key):
    base = jax.random.fold_in(key, 7)
    key_parts = jax.random.split(base, 3)
    group_count = N_SEQ // DOC_SHARDS
    offsets = jax.random.randint(key_parts[0], (BATCH,), 0, DOCMAX)
    spans = jnp.concatenate([jnp.full((BATCH, group_count - 1), DOCMAX, jnp.int32), (DOCMAX - offsets)[:, None].astype(jnp.int32)], axis=1)
    cuts = jax.random.randint(key_parts[1], (BATCH, group_count, DOC_SHARDS - 1), 0, spans[:, :, None] + 1)
    forced = jax.random.randint(key_parts[2], (BATCH,), 0, group_count - 1)
    chosen = jnp.arange(group_count, dtype=jnp.int32)[None, :] == forced[:, None]
    cuts = jnp.where(chosen[:, :, None], 0, cuts)
    cuts = jnp.sort(cuts, axis=-1)
    bounds = jnp.concatenate([jnp.zeros((BATCH, group_count, 1), jnp.int32), cuts.astype(jnp.int32), spans[:, :, None]], axis=-1)
    pieces = bounds[:, :, 1:] - bounds[:, :, :-1]
    lengths = jnp.concatenate([offsets[:, None].astype(jnp.int32), pieces.reshape(BATCH, group_count * DOC_SHARDS)], axis=1)
    return lengths.astype(jnp.int32)


def draw_lengths(key, part):
    return doc_layout(key)


def draw_queries(key, part):
    shape = (BATCH, SEQLEN, HEADS * HEAD_DIM)
    field = jnp.clip(jax.random.normal(jax.random.fold_in(key, 21), shape, jnp.float32), -4.0, 4.0)
    return field.astype(jnp.bfloat16)


def draw_keys(key, part):
    shape = (BATCH, SEQLEN, KV_HEADS * HEAD_DIM)
    field = jnp.clip(jax.random.normal(jax.random.fold_in(key, 22), shape, jnp.float32), -4.0, 4.0)
    return field.astype(jnp.bfloat16)


def raised(drawn, rng, source, target, blocks, factor):
    owner, partner = [(jnp.arange(drawn.shape[dim]) // (drawn.shape[dim] // blocks)).reshape([-1 if axis == dim else 1 for axis in range(drawn.ndim)]) for dim in (source, target)]
    chosen = jax.random.permutation(rng, blocks)[partner]
    strong = (owner == chosen) | (owner == (partner + blocks // 2) % blocks)
    return jnp.where(strong, factor * drawn, drawn)


def shard_levels(key, shape, shards, low, high):
    factor_of = 1.0
    for axis_at, shards_of in shards:
        heights = jax.random.uniform(jax.random.fold_in(jax.random.fold_in(key, 6), axis_at), (shards_of,), jnp.float32, low / len(shards), high / len(shards))
        factor_of = factor_of * jnp.repeat(jnp.exp(heights), shape[axis_at] // shards_of).reshape((-1,) + (1,) * (len(shape) - 1 - axis_at))
    return factor_of


def scatter_about(own_key, extent, scale, limit, cuts=(), kind=jnp.bfloat16):
    entries = scale * jax.random.normal(own_key, extent, jnp.float32)
    if cuts:
        entries = entries * shard_levels(own_key, extent, cuts, -0.22, 0.18)
    return jnp.clip(entries, -limit, limit).astype(kind)


def heavy_noise(key, dims, width, most, shards, heavy, kind=jnp.bfloat16):
    entries = width * jax.random.normal(key, dims, jnp.float32)
    if shards:
        entries = entries * shard_levels(key, dims, shards, -0.22, 0.18)
    return jnp.clip(raised(entries, jax.random.fold_in(key, 3), *heavy), -most, most).astype(kind)


def setup_inputs(seed: int = 0) -> dict:
    arg_keys = jax.random.split(jax.random.key(seed), 10)
    return {
        "queries": draw_queries(jax.random.fold_in(arg_keys[9], 71), 0),
        "keys": draw_keys(jax.random.fold_in(arg_keys[9], 71), 0),
        "values": scatter_about(arg_keys[2], (BATCH, SEQLEN, KV_HEADS * HEAD_DIM), 1.0, 4.0, ((0, 8), (1, 16), (2, 2))),
        "query_tangent": scatter_about(arg_keys[3], (BATCH, SEQLEN, HEADS * HEAD_DIM), 1.0, 4.0, ((0, 8), (1, 16), (2, 2))),
        "key_tangent": scatter_about(arg_keys[4], (BATCH, SEQLEN, KV_HEADS * HEAD_DIM), 1.0, 4.0, ((0, 8), (1, 16), (2, 2))),
        "value_tangent": scatter_about(arg_keys[5], (BATCH, SEQLEN, KV_HEADS * HEAD_DIM), 1.0, 4.0, ((0, 8), (1, 16), (2, 2))),
        "lengths": draw_lengths(jax.random.fold_in(arg_keys[9], 71), 0),
        "out_weight": scatter_about(arg_keys[7], (HEADS * HEAD_DIM, D), (HEADS * HEAD_DIM) ** -0.5, 0.125, ((0, 2),)),
        "cotangent": heavy_noise(arg_keys[8], (BATCH, SEQLEN, D), (BATCH * SEQLEN) ** -0.5, 0.0625, ((0, 8), (1, 16)), (1, 2, 16, 2.0)),
    }


def doc_numbers(lengths_row, count):
    ends = jnp.cumsum(lengths_row)
    positions = jnp.arange(count, dtype=jnp.int32)
    return jnp.sum((ends[None, :] <= positions[:, None]).astype(jnp.int32), axis=1)


def reference(queries, keys, values, query_tangent, key_tangent, value_tangent, lengths, out_weight, cotangent):
    group_ratio = HEADS // KV_HEADS
    score_scale = HEAD_DIM ** -0.5
    positions = jnp.arange(SEQLEN, dtype=jnp.int32)

    def split_query(array):
        return array.astype(jnp.float32).reshape(SEQLEN, KV_HEADS, group_ratio, HEAD_DIM).transpose(1, 2, 0, 3)

    def split_key(array):
        return array.astype(jnp.float32).reshape(SEQLEN, KV_HEADS, HEAD_DIM).transpose(1, 0, 2)

    def one_sequence(operands):
        query_seq, key_seq, value_seq, dquery_seq, dkey_seq, dvalue_seq, doc_lens = operands
        docs = doc_numbers(doc_lens, SEQLEN)
        allowed = (docs[:, None] == docs[None, :]) & (positions[None, :] <= positions[:, None])

        def one_group(group_ops):
            query_grp, dquery_grp, key_grp, value_grp, dkey_grp, dvalue_grp = group_ops
            scores = jnp.einsum('rtd,sd->rts', query_grp, key_grp) * score_scale
            tangent = (jnp.einsum('rtd,sd->rts', dquery_grp, key_grp) + jnp.einsum('rtd,sd->rts', query_grp, dkey_grp)) * score_scale
            scores = jnp.where(allowed[None], scores, -1e30)
            highest = jnp.max(scores, axis=-1, keepdims=True)
            weight = jnp.where(allowed[None], jnp.exp(scores - highest), 0.0)
            weighted_tangent = weight * tangent
            total = jnp.sum(weight, axis=-1)
            cross = jnp.sum(weighted_tangent, axis=-1)
            lower_bound = lax.optimization_barrier(weight.astype(jnp.bfloat16)).astype(jnp.float32)
            lower_bound_tangent = lax.optimization_barrier(weighted_tangent.astype(jnp.bfloat16)).astype(jnp.float32)
            running_total = jnp.einsum('rts,sd->rtd', lower_bound, value_grp)
            accum_tangent = jnp.einsum('rts,sd->rtd', lower_bound_tangent, value_grp) + jnp.einsum('rts,sd->rtd', lower_bound, dvalue_grp)
            output = running_total / total[..., None]
            return accum_tangent / total[..., None] - (cross / total)[..., None] * output

        result = lax.map(one_group, (split_query(query_seq), split_query(dquery_seq), split_key(key_seq),
                                     split_key(value_seq), split_key(dkey_seq), split_key(dvalue_seq)))
        return result.transpose(2, 0, 1, 3).reshape(SEQLEN, HEADS * HEAD_DIM).astype(jnp.bfloat16)

    douts = lax.map(one_sequence, (queries, keys, values, query_tangent, key_tangent, value_tangent, lengths))
    flat = douts.reshape(BATCH * SEQLEN, HEADS * HEAD_DIM)
    layer_tangent = jnp.dot(flat, out_weight, preferred_element_type=jnp.float32).astype(jnp.bfloat16)
    layer_tangent = layer_tangent.reshape(BATCH, SEQLEN, D)
    weight_hvp = lax.dot_general(cotangent.reshape(BATCH * SEQLEN, D), flat, (((0,), (0,)), ((), ())),
                                 preferred_element_type=jnp.float32)
    return layer_tangent, weight_hvp
```

```python
import jax
import jax.numpy as jnp
from jax import lax
from jax.experimental import pallas as pl
from jax.experimental.pallas import tpu as pltpu
from jax.sharding import PartitionSpec as P

HEAD_DIM = 128
TOK = 128
GROUPS = 2
RATIO = 4
NX = 4
NZ = 4
DP = 8
DOCS = 17
COLS = RATIO * HEAD_DIM
SLICE = 512
BF16 = jnp.bfloat16
F32 = jnp.float32
MESH = pl.DeviceIdType.MESH


def kernel(
    len_ref, q_hbm, k_hbm, v_hbm, dq_hbm, dk_hbm, dv_hbm, w_hbm, cot_hbm,
    lt_ref, hvp_ref,
    cot_v, cot_send, cot_all, dout, kv, relay, q_v, dq_v, w_v,
    part, part_in, sums, z_send, z_in, lt_send, lt_own, lt_in,
    load_sem, kv_load, z_s, z_r, x1_s, x1_r, x2_s, x2_r,
    cot_s, cot_r, own_sem, y_s, y_r, p_s, p_r, f_s, f_r,
    px_s, px_r, pz_s, pz_r, lt_s, lt_r,
):
    seq = lax.axis_index("seq")
    dp = lax.axis_index("dp")
    head = lax.axis_index("head")
    x = lax.rem(seq, NX)
    z = lax.div(seq, NX)
    core = lax.rem(dp, 2)

    def x_dev(k):
        return {"seq": z * NX + lax.rem(x + k, NX)}

    def z_dev(k):
        return {"seq": lax.rem(z + k, NZ) * NX + x}

    def d_at(k):
        return lax.rem(dp + k, DP)

    partner = dp + 1 - 2 * core

    def remote(src, dst, send, recv, device):
        return pltpu.make_async_remote_copy(
            src_ref=src, dst_ref=dst, send_sem=send, recv_sem=recv,
            device_id=device, device_id_type=MESH,
        )

    barrier = pltpu.get_barrier_semaphore()
    peers = [x_dev(k) for k in range(1, NX)] + [z_dev(k) for k in range(1, NZ)]
    peers += [{"dp": d_at(k)} for k in range(1, DP)] + [{"head": 1 - head}]
    for peer in peers:
        pl.semaphore_signal(barrier, inc=1, device_id=peer, device_id_type=MESH)

    loads = [
        pltpu.make_async_copy(src, dst, load_sem.at[i])
        for i, (src, dst) in enumerate(
            [(cot_hbm.at[0], cot_v), (q_hbm.at[0], q_v), (dq_hbm.at[0], dq_v), (w_hbm, w_v)]
        )
    ]
    cot_load, q_load, dq_load, w_load = loads
    cot_load.start()
    tensors = (k_hbm, dk_hbm, v_hbm, dv_hbm)

    def own(g, a):
        return tensors[a].at[0, :, pl.ds(g * HEAD_DIM, HEAD_DIM)]

    pieces = [(g, a) for g in range(GROUPS) for a in range(4)]
    kv_loads = {
        p: pltpu.make_async_copy(own(*p), kv.at[p[0], p[1], 2], kv_load.at[p[0], p[1]])
        for p in pieces
    }
    for p in pieces:
        kv_loads[p].start()
    q_load.start()
    dq_load.start()
    w_load.start()

    cot_load.wait()

    @pl.loop(0, NX * NZ)
    def _(s):
        first = pl.multiple_of(s * 256, 256)
        turned = cot_v[:, pl.ds(first, 256)].T
        row = pl.multiple_of((lax.rem(s, NX) * NZ + lax.div(s, NX)) * 32, 32)
        for d in range(DP):
            cot_send[d, pl.ds(row, 32), :] = turned[d * 32 : (d + 1) * 32]

    pl.semaphore_wait(barrier, len(peers))

    to_z = {
        p: remote(own(*p), relay.at[p[0], p[1]], z_s.at[p[0], p[1]], z_r.at[p[0], p[1]], z_dev(1))
        for p in pieces
    }

    def to_x(p, k, src):
        g, a = p
        send, recv = ((x1_s, x1_r), (x2_s, x2_r))[k - 1]
        return remote(src, kv.at[g, a, 2 - k], send.at[g, a], recv.at[g, a], x_dev(k))

    for p in pieces:
        @pl.when(x >= 2)
        def _():
            to_z[p].start()

        @pl.when(x < 3)
        def _():
            to_x(p, 1, own(*p)).start()

        @pl.when(x < 2)
        def _():
            to_x(p, 2, own(*p)).start()

    cot_copies = [
        remote(cot_send.at[d_at(k)], cot_all.at[dp], cot_s.at[k - 1], cot_r.at[k - 1], {"dp": d_at(k)})
        for k in range(1, DP)
    ]
    for copy in cot_copies:
        copy.start()
    cot_own = pltpu.make_async_copy(cot_send.at[dp], cot_all.at[dp], own_sem)
    cot_own.start()

    for p in pieces:
        @pl.when(x >= 2)
        def _():
            to_z[p].wait_recv()
            to_x(p, 2, relay.at[p[0], p[1]]).start()

        @pl.when(x == 3)
        def _():
            to_x(p, 1, relay.at[p[0], p[1]]).start()

    base = seq * TOK
    query_pos = lax.broadcasted_iota(jnp.int32, (TOK, 1), 0) + base
    start = jnp.zeros((TOK, 1), jnp.int32)
    end = jnp.int32(0)
    for i in range(DOCS):
        end = end + len_ref[0, i]
        start = jnp.where(query_pos >= end, jnp.maximum(start, end), start)
    key_pos = lax.broadcasted_iota(jnp.int32, (TOK, 3 * TOK), 1) + (base - 2 * TOK)
    allowed = ((key_pos >= start) & (key_pos <= query_pos))[None]

    q_load.wait()
    dq_load.wait()
    scale = HEAD_DIM ** (-0.5)
    nt = (((1,), (1,)), ((), ()))
    y_copies, p_copies = {}, {}
    for g in range(GROUPS):
        for a in range(4):
            kv_loads[g, a].wait()
            to_x((g, a), 1, relay.at[g, a]).wait_recv()
            to_x((g, a), 2, relay.at[g, a]).wait_recv()
        heads = [slice((g * RATIO + r) * HEAD_DIM, (g * RATIO + r + 1) * HEAD_DIM) for r in range(RATIO)]
        q = jnp.concatenate([q_v[:, h] for h in heads], axis=0)
        dq = jnp.concatenate([dq_v[:, h] for h in heads], axis=0)
        key, dkey, value, dvalue = (kv[g, a].reshape(3 * TOK, HEAD_DIM) for a in range(4))
        scores = lax.dot_general(q, key, nt, preferred_element_type=F32)
        tangent = lax.dot_general(
            jnp.concatenate([dq, q], axis=1), jnp.concatenate([key, dkey], axis=1), nt,
            preferred_element_type=F32,
        )
        scores = jnp.where(allowed, scores.reshape(RATIO, TOK, 3 * TOK) * scale, -1e30)
        high = jnp.max(scores, axis=-1, keepdims=True)
        weight = jnp.where(allowed, jnp.exp(scores - high), 0.0)
        weighted = weight * (tangent.reshape(RATIO, TOK, 3 * TOK) * scale)
        total = jnp.sum(weight, axis=-1, keepdims=True).reshape(RATIO * TOK, 1)
        cross = jnp.sum(weighted, axis=-1, keepdims=True).reshape(RATIO * TOK, 1)
        low = weight.astype(BF16).reshape(RATIO * TOK, 3 * TOK)
        low_tangent = weighted.astype(BF16).reshape(RATIO * TOK, 3 * TOK)
        both = jnp.dot(low, jnp.concatenate([value, dvalue], axis=1), preferred_element_type=F32)
        accum = both[:, :HEAD_DIM]
        accum_tangent = both[:, HEAD_DIM:] + jnp.dot(low_tangent, value, preferred_element_type=F32)
        inverse = 1.0 / total
        result = ((accum_tangent - (cross * inverse) * accum) * inverse).astype(BF16)
        for r in range(RATIO):
            dout[g, dp, :, r * HEAD_DIM : (r + 1) * HEAD_DIM] = result[r * TOK : (r + 1) * TOK]
        for k in range(1, 4):
            y_copies[g, k] = remote(
                dout.at[g, dp], dout.at[g, dp], y_s.at[g, k - 1], y_r.at[g, k - 1], {"dp": d_at(2 * k)}
            )
            y_copies[g, k].start()
        p_copies[g] = remote(dout.at[g, dp], dout.at[g, dp], p_s.at[g], p_r.at[g], {"dp": partner})
        p_copies[g].start()

    w_load.wait()
    rows = jnp.concatenate([dout[g, dp] for g in range(GROUPS)], axis=1)
    lt_copies = []
    for j in range(4):
        first = pl.multiple_of((1 - head) * 2048 + j * 512, 512)
        lt_send[j] = jnp.dot(rows, w_v[:, pl.ds(first, 512)], preferred_element_type=F32).astype(BF16)
        copy = remote(lt_send.at[j], lt_in.at[j], lt_s.at[j], lt_r.at[j], {"head": 1 - head})
        copy.start()
        lt_copies.append(copy)
    for j in range(4):
        first = pl.multiple_of(head * 2048 + j * 512, 512)
        lt_own[j] = jnp.dot(rows, w_v[:, pl.ds(first, 512)], preferred_element_type=F32)

    cot_own.wait()
    for copy in cot_copies:
        copy.wait_recv()
    f_copies, px_copies, pz_copies = {}, {}, {}
    for g in range(GROUPS):
        for k in range(1, 4):
            y_copies[g, k].wait_recv()
            source = d_at(DP - 2 * k)
            f_copies[g, k] = remote(
                dout.at[g, source], dout.at[g, source], f_s.at[g, k - 1], f_r.at[g, k - 1], {"dp": partner}
            )
            f_copies[g, k].start()
    for g in range(GROUPS):
        p_copies[g].wait_recv()
        for k in range(1, 4):
            f_copies[g, k].wait_recv()
        left = jnp.concatenate([cot_all[d] for d in range(DP)], axis=1)
        terms = jnp.dot(left, dout[g].reshape(DP * TOK, COLS), preferred_element_type=F32)
        for t in range(NX):
            part[g, t] = terms[t * 128 : (t + 1) * 128].astype(BF16)
        for k in range(1, NX):
            px_copies[g, k] = remote(
                part.at[g, lax.rem(x + k, NX)], part_in.at[g, k - 1],
                px_s.at[g, k - 1], px_r.at[g, k - 1], x_dev(k),
            )
            px_copies[g, k].start()

    for g in range(GROUPS):
        acc = part[g, x].astype(F32)
        for k in range(1, NX):
            px_copies[g, k].wait_recv()
            acc = acc + part_in[g, k - 1].astype(F32)
        sums[g] = acc.reshape(NZ, 32, COLS)
        z_send[g] = acc.astype(BF16).reshape(NZ, 32, COLS)
        for k in range(1, NZ):
            pz_copies[g, k] = remote(
                z_send.at[g, lax.rem(z + k, NZ)], z_in.at[g, k - 1],
                pz_s.at[g, k - 1], pz_r.at[g, k - 1], z_dev(k),
            )
            pz_copies[g, k].start()

    for j in range(4):
        lt_copies[j].wait_recv()
        lt_ref[0, :, j * 512 : (j + 1) * 512] = (lt_own[j] + lt_in[j].astype(F32)).astype(BF16)

    for g in range(GROUPS):
        acc = sums[g, z]
        for k in range(1, NZ):
            pz_copies[g, k].wait_recv()
            acc = acc + z_in[g, k - 1].astype(F32)
        hvp_ref[:, g * COLS : (g + 1) * COLS] = acc

    for p in pieces:
        @pl.when(x >= 2)
        def _():
            to_z[p].wait_send()

        for k in (1, 2):
            to_x(p, k, relay.at[p[0], p[1]]).wait_send()
    for copies in (y_copies, p_copies, f_copies, px_copies, pz_copies):
        for copy in copies.values():
            copy.wait_send()
    for copy in cot_copies + lt_copies:
        copy.wait_send()


def on_device(*args):
    lengths, others = args[6], args[:6] + args[7:]
    dma = pltpu.SemaphoreType.DMA
    vmem = pltpu.VMEM
    return pl.pallas_call(
        kernel,
        name="tangent",
        out_shape=(
            jax.ShapeDtypeStruct((1, TOK, 2048), BF16),
            jax.ShapeDtypeStruct((32, 1024), F32),
        ),
        in_specs=[pl.BlockSpec(memory_space=pltpu.SMEM)] + [pl.BlockSpec(memory_space=pl.ANY)] * 8,
        out_specs=(pl.BlockSpec(memory_space=vmem), pl.BlockSpec(memory_space=vmem)),
        scratch_shapes=[
            vmem((TOK, 4096), BF16),
            vmem((DP, SLICE, TOK), BF16),
            vmem((DP, SLICE, TOK), BF16),
            vmem((GROUPS, DP, TOK, COLS), BF16),
            vmem((GROUPS, 4, 3, TOK, HEAD_DIM), BF16),
            vmem((GROUPS, 4, TOK, HEAD_DIM), BF16),
            vmem((TOK, 1024), BF16),
            vmem((TOK, 1024), BF16),
            vmem((1024, 4096), BF16),
            vmem((GROUPS, NX, 128, COLS), BF16),
            vmem((GROUPS, NX - 1, 128, COLS), BF16),
            vmem((GROUPS, NZ, 32, COLS), F32),
            vmem((GROUPS, NZ, 32, COLS), BF16),
            vmem((GROUPS, NZ - 1, 32, COLS), BF16),
            vmem((4, TOK, 512), BF16),
            vmem((4, TOK, 512), F32),
            vmem((4, TOK, 512), BF16),
            dma((4,)),
            dma((GROUPS, 4)),
            dma((GROUPS, 4)),
            dma((GROUPS, 4)),
            dma((GROUPS, 4)),
            dma((GROUPS, 4)),
            dma((GROUPS, 4)),
            dma((GROUPS, 4)),
            dma((DP - 1,)),
            dma((DP - 1,)),
            dma,
            dma((GROUPS, 3)),
            dma((GROUPS, 3)),
            dma((GROUPS,)),
            dma((GROUPS,)),
            dma((GROUPS, 3)),
            dma((GROUPS, 3)),
            dma((GROUPS, NX - 1)),
            dma((GROUPS, NX - 1)),
            dma((GROUPS, NZ - 1)),
            dma((GROUPS, NZ - 1)),
            dma((4,)),
            dma((4,)),
        ],
        compiler_params=pltpu.CompilerParams(
            collective_id=0, has_side_effects=True, vmem_limit_bytes=60 * 1024 * 1024
        ),
    )(lengths, *others)


def solution(mesh):
    placed = (
        P("dp", "seq", "head"),
        P("dp", "seq", "head"),
        P("dp", "seq", "head"),
        P("dp", "seq", "head"),
        P("dp", "seq", "head"),
        P("dp", "seq", "head"),
        P("dp", None),
        P("head", None),
        P("dp", "seq", None),
    )
    return jax.shard_map(
        on_device,
        mesh=mesh,
        in_specs=placed,
        out_specs=(P("dp", "seq", "head"), P(("seq", "dp"), "head")),
        check_vma=False,
    )
```

```python
import jax
import jax.numpy as jnp
from jax import lax
from jax.experimental import pallas as pl
from jax.experimental.pallas import tpu as pltpu
from jax.sharding import PartitionSpec as P

HEAD_DIM = 128
TOK = 128
GROUPS = 2
RATIO = 4
NX = 4
NZ = 4
DP = 8
DOCS = 17
CHUNKS = 4
WIDTH = 256
SLICE = 512
BF16 = jnp.bfloat16
F32 = jnp.float32
MESH = pl.DeviceIdType.MESH


def kernel(
    len_ref, q_hbm, k_hbm, v_hbm, dq_hbm, dk_hbm, dv_hbm, w_hbm, cot_hbm,
    lt_ref, hvp_ref,
    cot_v, cot_send, cot_all, dout, kv, early, q_v, dq_v, w_v,
    part, part_in, sums, z_send, z_in, lt_send, lt_own, lt_in,
    load_sem, kv_load, near_s, near_r, far_s, far_r, side_s, cross_s, early_r,
    cot_s, cot_r, own_sem, y_s, y_r, pair_s, pair_r,
    px_s, px_r, pz_s, pz_r, lt_s, lt_r,
):
    seq = lax.axis_index("seq")
    dp = lax.axis_index("dp")
    head = lax.axis_index("head")
    x = lax.rem(seq, NX)
    z = lax.div(seq, NX)
    core = lax.rem(dp, 2)

    def x_dev(k):
        return {"seq": z * NX + lax.rem(x + k, NX)}

    def z_dev(k):
        return {"seq": lax.rem(z + k, NZ) * NX + x}

    def seq_dev(k):
        return {"seq": lax.rem(seq + k, NX * NZ)}

    def d_at(k):
        return lax.rem(dp + k, DP)

    partner = dp + 1 - 2 * core

    def remote(src, dst, send, recv, device):
        return pltpu.make_async_remote_copy(
            src_ref=src, dst_ref=dst, send_sem=send, recv_sem=recv,
            device_id=device, device_id_type=MESH,
        )

    barrier = pltpu.get_barrier_semaphore()
    peers = [x_dev(k) for k in range(1, NX)] + [z_dev(k) for k in range(1, NZ)]
    peers += [seq_dev(k) for k in (1, 2, 3, 13, 14, 15)]
    peers += [{"dp": d_at(k)} for k in range(1, DP)] + [{"head": 1 - head}]
    for peer in peers:
        pl.semaphore_signal(barrier, inc=1, device_id=peer, device_id_type=MESH)

    loads = [
        pltpu.make_async_copy(src, dst, load_sem.at[i])
        for i, (src, dst) in enumerate(
            [(cot_hbm.at[0], cot_v), (q_hbm.at[0], q_v), (dq_hbm.at[0], dq_v), (w_hbm, w_v)]
        )
    ]
    cot_load, q_load, dq_load, w_load = loads
    cot_load.start()
    tensors = (k_hbm, dk_hbm, v_hbm, dv_hbm)

    def own(g, a):
        return tensors[a].at[0, :, pl.ds(g * HEAD_DIM, HEAD_DIM)]

    pieces = [(g, a) for g in range(GROUPS) for a in range(4)]
    kv_loads = {
        p: pltpu.make_async_copy(own(*p), kv.at[p[0], p[1], 2], kv_load.at[p[0], p[1]])
        for p in pieces
    }
    for p in pieces:
        kv_loads[p].start()
    q_load.start()
    dq_load.start()

    def turn(first_step, last_step):
        @pl.loop(first_step, last_step)
        def _(s):
            first = pl.multiple_of(s * 256, 256)
            turned = cot_v[:, pl.ds(first, 256)].T
            row = pl.multiple_of((lax.rem(s, NX) * NZ + lax.div(s, NX)) * 32, 32)
            for d in range(DP):
                cot_send[d, pl.ds(row, 32), :] = turned[d * 32 : (d + 1) * 32]

    cot_load.wait()
    turn(0, 8)
    pl.semaphore_wait(barrier, len(peers))

    def near(g, a):
        return remote(own(g, a), kv.at[g, a, 1], near_s.at[g, a], near_r.at[g, a], seq_dev(1))

    def far(g, a):
        return remote(own(g, a), kv.at[g, a, 0], far_s.at[g, a], far_r.at[g, a], seq_dev(2))

    def onward(g, a):
        return remote(kv.at[g, a, 1], kv.at[g, a, 0], side_s.at[g, a], far_r.at[g, a], x_dev(1))

    def ahead(a, k, send):
        return remote(own(1, a), early.at[a], send.at[1, a], early_r.at[1, a], x_dev(k))

    def across_near(a):
        return remote(early.at[a], kv.at[1, a, 1], cross_s.at[1, a], near_r.at[1, a], z_dev(1))

    def across_far(a):
        return remote(early.at[a], kv.at[1, a, 0], cross_s.at[1, a], far_r.at[1, a], seq_dev(3))

    for a in range(4):
        @pl.when(x == 2)
        def _():
            far(0, a).start()

        near(0, a).start()

        @pl.when(x < 2)
        def _():
            far(0, a).start()

    for a in range(4):
        @pl.when(x == 3)
        def _():
            ahead(a, 1, near_s).start()

        @pl.when(x == 2)
        def _():
            ahead(a, 3, far_s).start()

        @pl.when(x < 3)
        def _():
            near(1, a).start()

    turn(8, 16)
    w_load.start()

    cot_copies = [
        remote(cot_send.at[d_at(k)], cot_all.at[dp], cot_s.at[k - 1], cot_r.at[k - 1], {"dp": d_at(k)})
        for k in range(1, DP)
    ]
    for copy in cot_copies:
        copy.start()
    cot_own = pltpu.make_async_copy(cot_send.at[dp], cot_all.at[dp], own_sem)
    cot_own.start()

    for a in range(4):
        @pl.when(x == 0)
        def _():
            ahead(a, 1, near_s).wait_recv()
            across_near(a).start()

        @pl.when(x == 1)
        def _():
            ahead(a, 3, far_s).wait_recv()
            across_far(a).start()

    base = seq * TOK
    query_pos = lax.broadcasted_iota(jnp.int32, (TOK, 1), 0) + base
    start = jnp.zeros((TOK, 1), jnp.int32)
    end = jnp.int32(0)
    for i in range(DOCS):
        end = end + len_ref[0, i]
        start = jnp.where(query_pos >= end, jnp.maximum(start, end), start)
    key_pos = lax.broadcasted_iota(jnp.int32, (TOK, 3 * TOK), 1) + (base - 2 * TOK)
    allowed = ((key_pos >= start) & (key_pos <= query_pos))[None]

    q_load.wait()
    dq_load.wait()
    scale = HEAD_DIM ** (-0.5)
    nt = (((1,), (1,)), ((), ()))
    y_copies, pair_copies = {}, {}

    def pair(c, k):
        ref = dout.at[c, d_at(DP - 2 * k)]
        pair_copies[c, k] = remote(ref, ref, pair_s.at[c, k], pair_r.at[c, k], {"dp": partner})
        pair_copies[c, k].start()

    for g in range(GROUPS):
        for a in range(4):
            near(g, a).wait_recv()

            @pl.when(x == 0)
            def _():
                onward(g, a).start()

        if g == 0:
            @pl.when(x < 2)
            def _():
                for a in range(4):
                    far(1, a).start()

        for a in range(4):
            kv_loads[g, a].wait()
            far(g, a).wait_recv()
        heads = [slice((g * RATIO + r) * HEAD_DIM, (g * RATIO + r + 1) * HEAD_DIM) for r in range(RATIO)]
        q = jnp.concatenate([q_v[:, h] for h in heads], axis=0)
        dq = jnp.concatenate([dq_v[:, h] for h in heads], axis=0)
        key, dkey, value, dvalue = (kv[g, a].reshape(3 * TOK, HEAD_DIM) for a in range(4))
        scores = lax.dot_general(q, key, nt, preferred_element_type=F32)
        tangent = lax.dot_general(
            jnp.concatenate([dq, q], axis=1), jnp.concatenate([key, dkey], axis=1), nt,
            preferred_element_type=F32,
        )
        scores = jnp.where(allowed, scores.reshape(RATIO, TOK, 3 * TOK) * scale, -1e30)
        high = jnp.max(scores, axis=-1, keepdims=True)
        weight = jnp.where(allowed, jnp.exp(scores - high), 0.0)
        weighted = weight * (tangent.reshape(RATIO, TOK, 3 * TOK) * scale)
        total = jnp.sum(weight, axis=-1, keepdims=True).reshape(RATIO * TOK, 1)
        cross = jnp.sum(weighted, axis=-1, keepdims=True).reshape(RATIO * TOK, 1)
        low = weight.astype(BF16).reshape(RATIO * TOK, 3 * TOK)
        low_tangent = weighted.astype(BF16).reshape(RATIO * TOK, 3 * TOK)
        both = jnp.dot(low, jnp.concatenate([value, dvalue], axis=1), preferred_element_type=F32)
        accum = both[:, :HEAD_DIM]
        accum_tangent = both[:, HEAD_DIM:] + jnp.dot(low_tangent, value, preferred_element_type=F32)
        inverse = 1.0 / total
        result = ((accum_tangent - (cross * inverse) * accum) * inverse).astype(BF16)
        for r in range(RATIO):
            h = g * RATIO + r
            column = (h % 2) * HEAD_DIM
            dout[h // 2, dp, :, column : column + HEAD_DIM] = result[r * TOK : (r + 1) * TOK]
        for c in (2 * g, 2 * g + 1):
            mine = dout.at[c, dp]
            for k in (2, 1, 3):
                y_copies[c, k] = remote(
                    mine, mine, y_s.at[c, k - 1], y_r.at[c, k - 1], {"dp": d_at(2 * k)}
                )
                y_copies[c, k].start()
            pair(c, 0)

    w_load.wait()
    rows = jnp.concatenate([dout[c, dp] for c in range(CHUNKS)], axis=1)
    lt_copies, px_copies, pz_copies = [], {}, {}

    def projected(side, j):
        first = pl.multiple_of(side * 2048 + j * 512, 512)
        return jnp.dot(rows, w_v[:, pl.ds(first, 512)], preferred_element_type=F32)

    def project_away(j):
        lt_send[j] = projected(1 - head, j).astype(BF16)
        copy = remote(lt_send.at[j], lt_in.at[j], lt_s.at[j], lt_r.at[j], {"head": 1 - head})
        copy.start()
        lt_copies.append(copy)

    def gather(c):
        for k in (1, 3, 2):
            y_copies[c, k].wait_recv()
            pair(c, k)

    def multiply(c):
        for k in range(4):
            pair_copies[c, k].wait_recv()
        left = jnp.concatenate([cot_all[d] for d in range(DP)], axis=1)
        terms = jnp.dot(left, dout[c].reshape(DP * TOK, WIDTH), preferred_element_type=F32)
        for t in range(NX):
            part[c, t] = terms[t * 128 : (t + 1) * 128].astype(BF16)
        for k in range(1, NX):
            px_copies[c, k] = remote(
                part.at[c, lax.rem(x + k, NX)], part_in.at[c, k - 1],
                px_s.at[c, k - 1], px_r.at[c, k - 1], x_dev(k),
            )
            px_copies[c, k].start()

    def sum_x(c):
        acc = part[c, x].astype(F32)
        for k in range(1, NX):
            px_copies[c, k].wait_recv()
            acc = acc + part_in[c, k - 1].astype(F32)
        sums[c] = acc.reshape(NZ, 32, WIDTH)
        z_send[c] = acc.astype(BF16).reshape(NZ, 32, WIDTH)
        for k in range(1, NZ):
            pz_copies[c, k] = remote(
                z_send.at[c, lax.rem(z + k, NZ)], z_in.at[c, k - 1],
                pz_s.at[c, k - 1], pz_r.at[c, k - 1], z_dev(k),
            )
            pz_copies[c, k].start()

    for j in range(4):
        project_away(j)
    gather(0)
    gather(1)
    cot_own.wait()
    for copy in cot_copies:
        copy.wait_recv()
    multiply(0)
    gather(2)
    multiply(1)
    gather(3)
    multiply(2)
    sum_x(0)
    multiply(3)
    sum_x(1)
    for j in range(4):
        lt_own[j] = projected(head, j)
    sum_x(2)
    sum_x(3)

    for j in range(4):
        lt_copies[j].wait_recv()
        lt_ref[0, :, j * 512 : (j + 1) * 512] = (lt_own[j] + lt_in[j].astype(F32)).astype(BF16)

    for c in range(CHUNKS):
        acc = sums[c, z]
        for k in range(1, NZ):
            pz_copies[c, k].wait_recv()
            acc = acc + z_in[c, k - 1].astype(F32)
        hvp_ref[:, c * WIDTH : (c + 1) * WIDTH] = acc

    for g, a in pieces:
        near(g, a).wait_send()

        @pl.when(x < 3)
        def _():
            far(g, a).wait_send()

        @pl.when(x == 0)
        def _():
            onward(g, a).wait_send()

    for a in range(4):
        @pl.when(x < 2)
        def _():
            across_near(a).wait_send()

    for copies in (y_copies, pair_copies, px_copies, pz_copies):
        for copy in copies.values():
            copy.wait_send()
    for copy in cot_copies + lt_copies:
        copy.wait_send()


def on_device(*args):
    lengths, others = args[6], args[:6] + args[7:]
    dma = pltpu.SemaphoreType.DMA
    vmem = pltpu.VMEM
    return pl.pallas_call(
        kernel,
        name="tangent",
        out_shape=(
            jax.ShapeDtypeStruct((1, TOK, 2048), BF16),
            jax.ShapeDtypeStruct((32, 1024), F32),
        ),
        in_specs=[pl.BlockSpec(memory_space=pltpu.SMEM)] + [pl.BlockSpec(memory_space=pl.ANY)] * 8,
        out_specs=(pl.BlockSpec(memory_space=vmem), pl.BlockSpec(memory_space=vmem)),
        scratch_shapes=[
            vmem((TOK, 4096), BF16),
            vmem((DP, SLICE, TOK), BF16),
            vmem((DP, SLICE, TOK), BF16),
            vmem((CHUNKS, DP, TOK, WIDTH), BF16),
            vmem((GROUPS, 4, 3, TOK, HEAD_DIM), BF16),
            vmem((4, TOK, HEAD_DIM), BF16),
            vmem((TOK, 1024), BF16),
            vmem((TOK, 1024), BF16),
            vmem((1024, 4096), BF16),
            vmem((CHUNKS, NX, 128, WIDTH), BF16),
            vmem((CHUNKS, NX - 1, 128, WIDTH), BF16),
            vmem((CHUNKS, NZ, 32, WIDTH), F32),
            vmem((CHUNKS, NZ, 32, WIDTH), BF16),
            vmem((CHUNKS, NZ - 1, 32, WIDTH), BF16),
            vmem((4, TOK, 512), BF16),
            vmem((4, TOK, 512), F32),
            vmem((4, TOK, 512), BF16),
            dma((4,)),
            *[dma((GROUPS, 4))] * 8,
            dma((DP - 1,)),
            dma((DP - 1,)),
            dma,
            *[dma((CHUNKS, 3))] * 2,
            *[dma((CHUNKS, 4))] * 2,
            *[dma((CHUNKS, 3))] * 4,
            dma((4,)),
            dma((4,)),
        ],
        compiler_params=pltpu.CompilerParams(
            collective_id=0, has_side_effects=True, vmem_limit_bytes=60 * 1024 * 1024
        ),
    )(lengths, *others)


def solution(mesh):
    placed = (
        P("dp", "seq", "head"),
        P("dp", "seq", "head"),
        P("dp", "seq", "head"),
        P("dp", "seq", "head"),
        P("dp", "seq", "head"),
        P("dp", "seq", "head"),
        P("dp", None),
        P("head", None),
        P("dp", "seq", None),
    )
    return jax.shard_map(
        on_device,
        mesh=mesh,
        in_specs=placed,
        out_specs=(P("dp", "seq", "head"), P(("seq", "dp"), "head")),
        check_vma=False,
    )
```

```python
import jax
import jax.numpy as jnp
from jax import lax
from jax.experimental import pallas as pl
from jax.experimental.pallas import tpu as pltpu
from jax.sharding import PartitionSpec as P

HEAD_DIM = 128
TOK = 128
GROUPS = 2
RATIO = 4
NX = 4
NZ = 4
DP = 8
DOCS = 17
CHUNKS = 4
WIDTH = 256
SLICE = 512
BF16 = jnp.bfloat16
F32 = jnp.float32
MESH = pl.DeviceIdType.MESH


def kernel(
    len_ref, q_hbm, k_hbm, v_hbm, dq_hbm, dk_hbm, dv_hbm, w_hbm, cot_hbm,
    lt_ref, hvp_ref,
    cot_v, cot_send, cot_all, dout, kv, early, q_v, dq_v, w_v,
    part, part_in, sums, z_send, z_in, lt_send, lt_own, lt_in,
    load_sem, kv_load, near_s, near_r, far_s, far_r, side_s, cross_s, early_r,
    cot_s, cot_r, own_sem, y_s, y_r, pair_s, pair_r,
    px_s, px_r, pz_s, pz_r, lt_s, lt_r,
):
    seq = lax.axis_index("seq")
    dp = lax.axis_index("dp")
    head = lax.axis_index("head")
    x = lax.rem(seq, NX)
    z = lax.div(seq, NX)
    core = lax.rem(dp, 2)

    def x_dev(k):
        return {"seq": z * NX + lax.rem(x + k, NX)}

    def z_dev(k):
        return {"seq": lax.rem(z + k, NZ) * NX + x}

    def seq_dev(k):
        return {"seq": lax.rem(seq + k, NX * NZ)}

    def d_at(k):
        return lax.rem(dp + k, DP)

    partner = dp + 1 - 2 * core

    def remote(src, dst, send, recv, device):
        return pltpu.make_async_remote_copy(
            src_ref=src, dst_ref=dst, send_sem=send, recv_sem=recv,
            device_id=device, device_id_type=MESH,
        )

    barrier = pltpu.get_barrier_semaphore()
    peers = [x_dev(k) for k in range(1, NX)] + [z_dev(k) for k in range(1, NZ)]
    peers += [seq_dev(k) for k in (1, 2, 3, 13, 14, 15)]
    peers += [{"dp": d_at(k)} for k in range(1, DP)] + [{"head": 1 - head}]
    for peer in peers:
        pl.semaphore_signal(barrier, inc=1, device_id=peer, device_id_type=MESH)

    loads = [
        pltpu.make_async_copy(src, dst, load_sem.at[i])
        for i, (src, dst) in enumerate(
            [(cot_hbm.at[0], cot_v), (q_hbm.at[0], q_v), (dq_hbm.at[0], dq_v), (w_hbm, w_v)]
        )
    ]
    cot_load, q_load, dq_load, w_load = loads
    cot_load.start()
    tensors = (k_hbm, dk_hbm, v_hbm, dv_hbm)

    def own(g, a):
        return tensors[a].at[0, :, pl.ds(g * HEAD_DIM, HEAD_DIM)]

    pieces = [(g, a) for g in range(GROUPS) for a in range(4)]
    kv_loads = {
        p: pltpu.make_async_copy(own(*p), kv.at[p[0], p[1], 2], kv_load.at[p[0], p[1]])
        for p in pieces
    }
    for p in pieces:
        kv_loads[p].start()
    q_load.start()
    dq_load.start()

    def turn(first_step, last_step):
        @pl.loop(first_step, last_step)
        def _(s):
            first = pl.multiple_of(s * 256, 256)
            turned = cot_v[:, pl.ds(first, 256)].T
            row = pl.multiple_of((lax.rem(s, NX) * NZ + lax.div(s, NX)) * 32, 32)
            for d in range(DP):
                cot_send[d, pl.ds(row, 32), :] = turned[d * 32 : (d + 1) * 32]

    cot_load.wait()
    turn(0, 8)
    pl.semaphore_wait(barrier, len(peers))

    def near(g, a):
        return remote(own(g, a), kv.at[g, a, 1], near_s.at[g, a], near_r.at[g, a], seq_dev(1))

    def far(g, a):
        return remote(own(g, a), kv.at[g, a, 0], far_s.at[g, a], far_r.at[g, a], seq_dev(2))

    def onward(g, a):
        return remote(kv.at[g, a, 1], kv.at[g, a, 0], side_s.at[g, a], far_r.at[g, a], x_dev(1))

    def ahead(a, k, send):
        return remote(own(1, a), early.at[a], send.at[1, a], early_r.at[1, a], x_dev(k))

    def across_near(a):
        return remote(early.at[a], kv.at[1, a, 1], cross_s.at[1, a], near_r.at[1, a], z_dev(1))

    def across_far(a):
        return remote(early.at[a], kv.at[1, a, 0], cross_s.at[1, a], far_r.at[1, a], seq_dev(3))

    for a in range(4):
        @pl.when(x == 2)
        def _():
            far(0, a).start()

        near(0, a).start()

        @pl.when(x < 2)
        def _():
            far(0, a).start()

    for a in range(4):
        @pl.when(x == 3)
        def _():
            ahead(a, 1, near_s).start()

        @pl.when(x == 2)
        def _():
            ahead(a, 3, far_s).start()

        @pl.when(x < 3)
        def _():
            near(1, a).start()

    turn(8, 16)
    w_load.start()

    cot_copies = [
        remote(cot_send.at[d_at(k)], cot_all.at[dp], cot_s.at[k - 1], cot_r.at[k - 1], {"dp": d_at(k)})
        for k in range(1, DP)
    ]
    for copy in cot_copies:
        copy.start()
    cot_own = pltpu.make_async_copy(cot_send.at[dp], cot_all.at[dp], own_sem)
    cot_own.start()

    for a in range(4):
        @pl.when(x == 0)
        def _():
            ahead(a, 1, near_s).wait_recv()
            across_near(a).start()

        @pl.when(x == 1)
        def _():
            ahead(a, 3, far_s).wait_recv()
            across_far(a).start()

    base = seq * TOK
    query_pos = lax.broadcasted_iota(jnp.int32, (TOK, 1), 0) + base
    start = jnp.zeros((TOK, 1), jnp.int32)
    end = jnp.int32(0)
    for i in range(DOCS):
        end = end + len_ref[0, i]
        start = jnp.where(query_pos >= end, jnp.maximum(start, end), start)
    key_pos = lax.broadcasted_iota(jnp.int32, (TOK, 3 * TOK), 1) + (base - 2 * TOK)
    allowed = ((key_pos >= start) & (key_pos <= query_pos))[None]

    q_load.wait()
    dq_load.wait()
    scale = HEAD_DIM ** (-0.5)
    nt = (((1,), (1,)), ((), ()))
    y_copies, pair_copies = {}, {}

    def pair(c, k):
        ref = dout.at[c, d_at(DP - 2 * k)]
        pair_copies[c, k] = remote(ref, ref, pair_s.at[c, k], pair_r.at[c, k], {"dp": partner})
        pair_copies[c, k].start()

    for g in range(GROUPS):
        for a in range(4):
            near(g, a).wait_recv()

            @pl.when(x == 0)
            def _():
                onward(g, a).start()

        if g == 0:
            @pl.when(x < 2)
            def _():
                for a in range(4):
                    far(1, a).start()

        for a in range(4):
            kv_loads[g, a].wait()
            far(g, a).wait_recv()
        heads = [slice((g * RATIO + r) * HEAD_DIM, (g * RATIO + r + 1) * HEAD_DIM) for r in range(RATIO)]
        q = jnp.concatenate([q_v[:, h] for h in heads], axis=0)
        dq = jnp.concatenate([dq_v[:, h] for h in heads], axis=0)
        key, dkey, value, dvalue = (kv[g, a].reshape(3 * TOK, HEAD_DIM) for a in range(4))
        scores = lax.dot_general(q, key, nt, preferred_element_type=F32)
        tangent = lax.dot_general(
            jnp.concatenate([dq, q], axis=1), jnp.concatenate([key, dkey], axis=1), nt,
            preferred_element_type=F32,
        )
        scores = jnp.where(allowed, scores.reshape(RATIO, TOK, 3 * TOK) * scale, -1e30)
        high = jnp.max(scores, axis=-1, keepdims=True)
        weight = jnp.where(allowed, jnp.exp(scores - high), 0.0)
        weighted = weight * (tangent.reshape(RATIO, TOK, 3 * TOK) * scale)
        total = jnp.sum(weight, axis=-1, keepdims=True).reshape(RATIO * TOK, 1)
        cross = jnp.sum(weighted, axis=-1, keepdims=True).reshape(RATIO * TOK, 1)
        low = weight.astype(BF16).reshape(RATIO * TOK, 3 * TOK)
        low_tangent = weighted.astype(BF16).reshape(RATIO * TOK, 3 * TOK)
        both = jnp.dot(low, jnp.concatenate([value, dvalue], axis=1), preferred_element_type=F32)
        accum = both[:, :HEAD_DIM]
        accum_tangent = both[:, HEAD_DIM:] + jnp.dot(low_tangent, value, preferred_element_type=F32)
        inverse = 1.0 / total
        result = ((accum_tangent - (cross * inverse) * accum) * inverse).astype(BF16)
        for r in range(RATIO):
            h = g * RATIO + r
            column = (h % 2) * HEAD_DIM
            dout[h // 2, dp, :, column : column + HEAD_DIM] = result[r * TOK : (r + 1) * TOK]
        for c in (2 * g, 2 * g + 1):
            mine = dout.at[c, dp]
            for k in (2, 1, 3):
                y_copies[c, k] = remote(
                    mine, mine, y_s.at[c, k - 1], y_r.at[c, k - 1], {"dp": d_at(2 * k)}
                )
                y_copies[c, k].start()
            pair(c, 0)

    w_load.wait()
    rows = jnp.concatenate([dout[c, dp] for c in range(CHUNKS)], axis=1)
    lt_copies, px_copies, pz_copies = [], {}, {}

    def projected(side, j):
        first = pl.multiple_of(side * 2048 + j * 512, 512)
        return jnp.dot(rows, w_v[:, pl.ds(first, 512)], preferred_element_type=F32)

    def project_away(j):
        lt_send[j] = projected(1 - head, j).astype(BF16)
        copy = remote(lt_send.at[j], lt_in.at[j], lt_s.at[j], lt_r.at[j], {"head": 1 - head})
        copy.start()
        lt_copies.append(copy)

    def gather(c):
        for k in (1, 3, 2):
            y_copies[c, k].wait_recv()
            pair(c, k)

    def multiply(c):
        for k in range(4):
            pair_copies[c, k].wait_recv()
        left = jnp.concatenate([cot_all[d] for d in range(DP)], axis=1)
        terms = jnp.dot(left, dout[c].reshape(DP * TOK, WIDTH), preferred_element_type=F32)
        for t in range(NX):
            part[c, t] = terms[t * 128 : (t + 1) * 128].astype(BF16)
        for k in range(1, NX):
            px_copies[c, k] = remote(
                part.at[c, lax.rem(x + k, NX)], part_in.at[c, k - 1],
                px_s.at[c, k - 1], px_r.at[c, k - 1], x_dev(k),
            )
            px_copies[c, k].start()

    def sum_x(c):
        acc = part[c, x].astype(F32)
        for k in range(1, NX):
            px_copies[c, k].wait_recv()
            acc = acc + part_in[c, k - 1].astype(F32)
        sums[c] = acc.reshape(NZ, 32, WIDTH)
        z_send[c] = acc.astype(BF16).reshape(NZ, 32, WIDTH)
        for k in range(1, NZ):
            pz_copies[c, k] = remote(
                z_send.at[c, lax.rem(z + k, NZ)], z_in.at[c, k - 1],
                pz_s.at[c, k - 1], pz_r.at[c, k - 1], z_dev(k),
            )
            pz_copies[c, k].start()

    for j in range(4):
        project_away(j)
    gather(0)
    gather(1)
    cot_own.wait()
    for copy in cot_copies:
        copy.wait_recv()
    multiply(0)
    gather(2)
    multiply(1)
    gather(3)
    multiply(2)
    sum_x(0)
    multiply(3)
    sum_x(1)
    for j in range(4):
        lt_own[j] = projected(head, j)
    sum_x(2)
    sum_x(3)

    for j in range(4):
        lt_copies[j].wait_recv()
        lt_ref[0, :, j * 512 : (j + 1) * 512] = (lt_own[j] + lt_in[j].astype(F32)).astype(BF16)

    for c in range(CHUNKS):
        acc = sums[c, z]
        for k in range(1, NZ):
            pz_copies[c, k].wait_recv()
            acc = acc + z_in[c, k - 1].astype(F32)
        hvp_ref[:, c * WIDTH : (c + 1) * WIDTH] = acc

    for g, a in pieces:
        near(g, a).wait_send()

        @pl.when(x < 3)
        def _():
            far(g, a).wait_send()

        @pl.when(x == 0)
        def _():
            onward(g, a).wait_send()

    for a in range(4):
        @pl.when(x < 2)
        def _():
            across_near(a).wait_send()

    for copies in (y_copies, pair_copies, px_copies, pz_copies):
        for copy in copies.values():
            copy.wait_send()
    for copy in cot_copies + lt_copies:
        copy.wait_send()


def hand_over(lt_in, hvp_in, lt_out, hvp_out, lt_v, hvp_v, in_sem, out_sem):
    steps = []
    for i in range(4):
        rows = pl.ds(i * 32, 32)
        steps.append((lt_in.at[0, rows], lt_v.at[rows], lt_out.at[0, rows]))
    steps.append((hvp_in, hvp_v, hvp_out))
    fetched = [pltpu.make_async_copy(a, b, in_sem.at[i]) for i, (a, b, _) in enumerate(steps)]
    stored = [pltpu.make_async_copy(b, c, out_sem.at[i]) for i, (_, b, c) in enumerate(steps)]
    for copy in fetched:
        copy.start()
    for first, second in zip(fetched, stored):
        first.wait()
        second.start()
    for copy in stored:
        copy.wait()


def on_device(*args):
    lengths, others = args[6], args[:6] + args[7:]
    dma = pltpu.SemaphoreType.DMA
    vmem = pltpu.VMEM
    shapes = (
        jax.ShapeDtypeStruct((1, TOK, 2048), BF16),
        jax.ShapeDtypeStruct((32, 1024), F32),
    )
    results = pl.pallas_call(
        kernel,
        name="tangent",
        out_shape=shapes,
        in_specs=[pl.BlockSpec(memory_space=pltpu.SMEM)] + [pl.BlockSpec(memory_space=pl.ANY)] * 8,
        out_specs=(pl.BlockSpec(memory_space=vmem), pl.BlockSpec(memory_space=vmem)),
        scratch_shapes=[
            vmem((TOK, 4096), BF16),
            vmem((DP, SLICE, TOK), BF16),
            vmem((DP, SLICE, TOK), BF16),
            vmem((CHUNKS, DP, TOK, WIDTH), BF16),
            vmem((GROUPS, 4, 3, TOK, HEAD_DIM), BF16),
            vmem((4, TOK, HEAD_DIM), BF16),
            vmem((TOK, 1024), BF16),
            vmem((TOK, 1024), BF16),
            vmem((1024, 4096), BF16),
            vmem((CHUNKS, NX, 128, WIDTH), BF16),
            vmem((CHUNKS, NX - 1, 128, WIDTH), BF16),
            vmem((CHUNKS, NZ, 32, WIDTH), F32),
            vmem((CHUNKS, NZ, 32, WIDTH), BF16),
            vmem((CHUNKS, NZ - 1, 32, WIDTH), BF16),
            vmem((4, TOK, 512), BF16),
            vmem((4, TOK, 512), F32),
            vmem((4, TOK, 512), BF16),
            dma((4,)),
            *[dma((GROUPS, 4))] * 8,
            dma((DP - 1,)),
            dma((DP - 1,)),
            dma,
            *[dma((CHUNKS, 3))] * 2,
            *[dma((CHUNKS, 4))] * 2,
            *[dma((CHUNKS, 3))] * 4,
            dma((4,)),
            dma((4,)),
        ],
        compiler_params=pltpu.CompilerParams(
            collective_id=0, has_side_effects=True, vmem_limit_bytes=60 * 1024 * 1024
        ),
    )(lengths, *others)
    anywhere = pl.BlockSpec(memory_space=pl.ANY)
    return pl.pallas_call(
        hand_over,
        name="hand_over",
        out_shape=shapes,
        in_specs=[anywhere] * 2,
        out_specs=(anywhere, anywhere),
        scratch_shapes=[vmem((TOK, 2048), BF16), vmem((32, 1024), F32), dma((5,)), dma((5,))],
    )(*results)


def solution(mesh):
    placed = (
        P("dp", "seq", "head"),
        P("dp", "seq", "head"),
        P("dp", "seq", "head"),
        P("dp", "seq", "head"),
        P("dp", "seq", "head"),
        P("dp", "seq", "head"),
        P("dp", None),
        P("head", None),
        P("dp", "seq", None),
    )
    return jax.shard_map(
        on_device,
        mesh=mesh,
        in_specs=placed,
        out_specs=(P("dp", "seq", "head"), P(("seq", "dp"), "head")),
        check_vma=False,
    )
```
